32 devices in a mesh: row: 4 (over y, core), col: 8 (over z, x).
Axes of the slice: x: 2, y: 2, z: 4, core: 2. Of those that a mesh axis runs over, the one named last changes fastest.
Arguments:
- observed: float32 [2048, 128], P(('row', 'col')), may hold values from -60 to 60
- lengths: int32 [2048], P(('row', 'col')), may hold values from 0 to 128
- features: float32 [2048, 32], P(('row', 'col')), may hold values from -6 to 6
- length_scale: float32 [32], replicated, may hold values from 2 to 5
- epoch_gain: float32 [128], replicated, may hold values from 0.5 to 2
Outputs:
- solution_field: float32 [2048, 128], P(('row', 'col'))
- residual: float32 [2048, 128], P(('row', 'col'))
The draws below stay inside these ranges and needn't reach their ends.
All inputs are finite; a program needn't handle non-finite values.
Results may differ from the reference program's by a relative error of at most 0.007.
Values may be sent and summed in bfloat16 or wider, within the bound.
A program may use at most 64 MiB of HBM per device.

```python
import math
import jax
import jax.numpy as jnp
from jax import lax

E = 128
F = 32
ITERS = 2
N_TRIALS = 2048


def draw_observed(key, part):
    rows = jnp.arange(N_TRIALS).astype(jnp.float32)
    rise = 1.0 + 2.0 * rows / max(N_TRIALS - 1, 1)
    values = jnp.clip(jax.random.normal(key, (N_TRIALS, E), jnp.float32), -4.0, 4.0)
    return values * rise[:, None]


def touch_ends(drawn, stream_key, least, top_value):
    longest = drawn.shape.index(max(drawn.shape))
    spots = []
    for shift in (0, 1):
        where = [jax.random.randint(jax.random.fold_in(stream_key, axis), (), 0, length) for axis, length in enumerate(drawn.shape)]
        where[longest] = (where[longest] + shift) % drawn.shape[longest]
        spots.append(tuple(where))
    return drawn.at[spots[0]].set(least).at[spots[1]].set(top_value)


def levels(key, dims, cuts, low, top_value):
    def one(axis_at, blocks):
        steps = jax.random.uniform(jax.random.fold_in(jax.random.fold_in(key, 6), axis_at), (blocks,), jnp.float32, low / len(cuts), top_value / len(cuts))
        return jnp.repeat(jnp.exp(steps), dims[axis_at] // blocks).reshape((-1,) + (1,) * (len(dims) - axis_at - 1))

    gain = one(*cuts[0])
    for cut in cuts[1:]:
        gain = gain * one(*cut)
    return gain


def normal_values(key, shape, width, limit, cuts=(), kind=jnp.bfloat16):
    loudness = levels(key, shape, cuts, -0.22, 0.18) if cuts else 1.0
    result = jax.random.normal(key, shape, jnp.float32) * width * loudness
    return jnp.minimum(jnp.maximum(result, -limit), limit).astype(kind)


def setup_inputs(seed: int = 0) -> dict:
    seeds = jax.random.split(jax.random.key(seed), 6)
    observed = draw_observed(jax.random.fold_in(seeds[5], 71), 0)
    lengths = touch_ends(jax.random.randint(seeds[1], (N_TRIALS,), 0, E + 1), jax.random.fold_in(seeds[1], 1), 0, E).astype(jnp.int32)
    features = normal_values(seeds[2], (N_TRIALS, F), 1.0, 6.0, ((0, 32),), jnp.float32)
    length_scale = jnp.clip(jnp.exp(jax.random.uniform(seeds[3], (F,), jnp.float32, math.log(2.0), math.log(5.0))), 2.0, 5.0)
    epoch_gain = jnp.clip(jnp.exp(jax.random.uniform(seeds[4], (E,), jnp.float32, math.log(0.5), math.log(2.0))), 0.5, 2.0)
    return {"observed": observed, "lengths": lengths, "features": features, "length_scale": length_scale, "epoch_gain": epoch_gain}


noise_level = 0.3
epoch_offset = 16.0


def epoch_matrix(epoch_gain):
    steps = jnp.arange(E).astype(jnp.float32)
    base = epoch_offset / (steps[:, None] + steps[None, :] + epoch_offset)
    return base + jnp.diag(epoch_gain)


def kernel_block(left, left_sq, right, right_sq):
    cross = jnp.dot(left, right.T, precision=lax.Precision.HIGHEST, preferred_element_type=jnp.float32)
    dist = jnp.maximum(left_sq[:, None] + right_sq[None, :] - 2.0 * cross, 0.0)
    return jnp.exp(-0.5 * dist).astype(jnp.bfloat16)


def reference(observed, lengths, features, length_scale, epoch_gain):
    scaled = features / length_scale[None, :]
    sq = jnp.sum(scaled * scaled, axis=1)
    mask = (jnp.arange(E)[None, :] < lengths[:, None]).astype(jnp.float32)
    epoch_kernel = epoch_matrix(epoch_gain)
    block = min(512, N_TRIALS)
    count = N_TRIALS // block

    def operate(field):
        mixed = jnp.dot(mask * field, epoch_kernel, precision=lax.Precision.HIGHEST,
                        preferred_element_type=jnp.float32).astype(jnp.bfloat16)

        def one_block(index):
            start = (index * block).astype(jnp.int32)
            left = lax.dynamic_slice_in_dim(scaled, start, block, 0)
            left_sq = lax.dynamic_slice_in_dim(sq, start, block, 0)
            return jnp.dot(kernel_block(left, left_sq, scaled, sq), mixed, preferred_element_type=jnp.float32)

        product = lax.map(one_block, jnp.arange(count, dtype=jnp.int32)).reshape(N_TRIALS, E)
        return mask * product + noise_level * field

    solution_field = jnp.zeros_like(observed)
    residual = mask * observed
    direction = residual
    norm_now = jnp.sum(residual * residual)
    for step in range(ITERS):
        image = operate(direction)
        alpha = norm_now / jnp.sum(direction * image)
        solution_field = solution_field + alpha * direction
        residual = residual - alpha * image
        norm_next = jnp.sum(residual * residual)
        direction = residual + (norm_next / norm_now) * direction
        norm_now = norm_next
    return solution_field, residual
```

```python
import functools

import jax
import jax.numpy as jnp
from jax import lax
from jax.experimental import pallas as pl
from jax.experimental.pallas import tpu as pltpu
from jax.sharding import PartitionSpec as P

noise_level = 0.3
epoch_offset = 16.0
HIGHEST = lax.Precision.HIGHEST
SEND = jnp.bfloat16


def solve_kernel(n_row, n_col, obs_ref, len_ref, feat_ref, scale_ref, gain_ref,
                 sol_ref, res_ref,
                 right, left, wbuf, kmat, psend, precv, ssend, srow, scol,
                 feat_sem, left_sem, w_sem, p_sem, srow_sem, scol_sem):
    rows, width = obs_ref.shape
    features = feat_ref.shape[1]
    pack = width // features
    sub = rows // pack
    my_row = lax.axis_index("row")
    my_col = lax.axis_index("col")

    def row_peer(shift):
        return {"row": lax.rem(my_row + shift, n_row)}

    def col_peer(shift):
        return {"col": lax.rem(my_col + shift, n_col)}

    def put(src, dst, sems, peer):
        copy = pltpu.make_async_remote_copy(
            src_ref=src, dst_ref=dst, send_sem=sems.at[0], recv_sem=sems.at[1],
            device_id=peer, device_id_type=pl.DeviceIdType.MESH)
        copy.start()
        return copy

    barrier = pltpu.get_barrier_semaphore()
    for shift in range(1, n_row):
        pl.semaphore_signal(barrier, inc=1, device_id=row_peer(shift), device_id_type=pl.DeviceIdType.MESH)
    for shift in range(1, n_col):
        pl.semaphore_signal(barrier, inc=1, device_id=col_peer(shift), device_id_type=pl.DeviceIdType.MESH)

    scaled = feat_ref[...] / scale_ref[...]
    packed = jnp.concatenate([scaled[k * sub:(k + 1) * sub] for k in range(pack)], axis=1)
    right[0] = packed
    left[0] = packed

    at_row = lax.broadcasted_iota(jnp.int32, (rows, rows), 0)
    at_col = lax.broadcasted_iota(jnp.int32, (rows, rows), 1)
    spread = jnp.where(at_row == at_col, len_ref[...].astype(jnp.float32), 0.0)
    lengths = jnp.sum(spread, axis=1, keepdims=True)
    epoch = lax.broadcasted_iota(jnp.int32, (rows, width), 1).astype(jnp.float32)
    mask = (epoch < lengths).astype(jnp.float32)

    s = lax.broadcasted_iota(jnp.int32, (width, width), 0)
    t = lax.broadcasted_iota(jnp.int32, (width, width), 1)
    epoch_kernel = epoch_offset / ((s + t).astype(jnp.float32) + epoch_offset)
    epoch_kernel = epoch_kernel + jnp.where(s == t, gain_ref[...], 0.0)

    def mix(field):
        return jnp.dot(mask * field, epoch_kernel, precision=HIGHEST,
                       preferred_element_type=jnp.float32).astype(jnp.bfloat16)

    res0 = mask * obs_ref[...]
    wbuf[0, 0] = mix(res0)

    pl.semaphore_wait(barrier, n_row - 1 + n_col - 1)

    pending = []
    right_copies = [put(right.at[0], right.at[d], feat_sem.at[d], col_peer(d)) for d in range(1, n_col)]
    left_copies = [put(left.at[0], left.at[d], left_sem.at[d], row_peer(d)) for d in range(1, n_row)]

    def send_w(step):
        return [put(wbuf.at[step, 0], wbuf.at[step, d], w_sem.at[step, d], col_peer(d)) for d in range(1, n_col)]

    w_copies = send_w(0)

    for copy in left_copies + right_copies:
        copy.wait_recv()
    pending += left_copies + right_copies

    lefts = left[...].reshape(n_row * sub, width)
    rolls = [lefts] + [pltpu.roll(lefts, k * features, 1) for k in range(1, pack)]
    group = lax.broadcasted_iota(jnp.int32, (sub, width), 1) // features
    stacked = []
    for k in range(pack):
        for d in range(n_row):
            for q in range(pack):
                piece = rolls[(k - q) % pack][d * sub:(d + 1) * sub]
                stacked.append(jnp.where(group == k, piece, 0.0))
    stacked = jnp.concatenate(stacked, axis=0)
    block = n_row * rows
    rights = right[...].reshape(n_col * sub, width)
    over = (((1,), (1,)), ((), ()))
    first = stacked[:block]
    left_sq = jnp.sum(first * first, axis=1, keepdims=True)
    picks_at = lax.broadcasted_iota(jnp.int32, (8, width), 0)
    picks = (lax.broadcasted_iota(jnp.int32, (8, width), 1) // features == picks_at).astype(jnp.float32)
    right_sq = lax.dot_general(picks, rights * rights, over, precision=HIGHEST,
                               preferred_element_type=jnp.float32)
    cross = lax.dot_general(stacked, rights, over, precision=HIGHEST,
                            preferred_element_type=jnp.float32)
    span = n_col * sub
    for k in range(pack):
        dist = jnp.maximum(left_sq + right_sq[k:k + 1] - 2.0 * cross[k * block:(k + 1) * block], 0.0)
        kmat[:, k * span:(k + 1) * span] = jnp.exp(-0.5 * dist).astype(jnp.bfloat16)

    def spread_product(step, copies):
        for copy in copies:
            copy.wait_recv()
        pieces = [wbuf[step, d, k * sub:(k + 1) * sub] for k in range(pack) for d in range(n_col)]
        part = jnp.dot(kmat[...], jnp.concatenate(pieces, axis=0), preferred_element_type=jnp.float32)
        sends = []
        for d in range(1, n_row):
            psend[step, d] = part[d * rows:(d + 1) * rows].astype(SEND)
            sends.append(put(psend.at[step, d], precv.at[step, d], p_sem.at[step, d], row_peer(n_row - d)))
        return part[:rows], sends

    def collect(step, own, sends):
        total = own
        for d, copy in enumerate(sends, 1):
            copy.wait_recv()
            total = total + precv[step, d].astype(jnp.float32)
        return total

    lane_row = lax.broadcasted_iota(jnp.int32, (8, width), 0)

    def start_sums(step, one, two):
        one = jnp.sum(one, axis=0, keepdims=True)
        two = jnp.sum(two, axis=0, keepdims=True)
        srow[step, 0] = jnp.where(lane_row == 0, one, jnp.where(lane_row == 1, two, 0.0))
        return [put(srow.at[step, 0], srow.at[step, d], srow_sem.at[step, d], row_peer(d)) for d in range(1, n_row)]

    def relay_sums(step, copies):
        for copy in copies:
            copy.wait_recv()
        scol[step, 0] = jnp.sum(srow[step], axis=0)
        return [put(scol.at[step, 0], scol.at[step, d], scol_sem.at[step, d], col_peer(d)) for d in range(1, n_col)]

    def finish_sums(step, copies):
        for copy in copies:
            copy.wait_recv()
        total = jnp.sum(jnp.sum(scol[step], axis=0), axis=1, keepdims=True)
        return total[0:1], total[1:2]

    own, p_copies = spread_product(0, w_copies)
    pending += w_copies + p_copies
    image0 = mask * collect(0, own, p_copies) + noise_level * res0
    wbuf[1, 0] = mix(image0)
    w_copies = send_w(1)
    row_copies = start_sums(0, res0 * res0, res0 * image0)
    col_copies = relay_sums(0, row_copies)
    pending += w_copies + row_copies + col_copies
    own, p_copies = spread_product(1, w_copies)
    pending += p_copies
    norm0, curve0 = finish_sums(0, col_copies)
    alpha0 = norm0 / curve0
    res1 = res0 - alpha0 * image0
    image00 = mask * collect(1, own, p_copies) + noise_level * image0
    image1 = image0 - alpha0 * image00
    row_copies = start_sums(1, res1 * res1, res1 * image1)
    col_copies = relay_sums(1, row_copies)
    pending += row_copies + col_copies
    norm1, curve1 = finish_sums(1, col_copies)
    ratio = norm1 / norm0
    alpha1 = norm1 / (curve1 - ratio * norm1 / alpha0)
    sol_ref[...] = alpha0 * res0 + alpha1 * (res1 + ratio * res0)
    res_ref[...] = res1 - alpha1 * (image1 + ratio * image0)
    for copy in pending:
        copy.wait_send()


def solution(mesh):
    n_row, n_col = mesh.shape["row"], mesh.shape["col"]

    def per_device(observed, lengths, features, length_scale, epoch_gain):
        rows, width = observed.shape
        count = features.shape[1]
        sub = rows * count // width
        dma = pltpu.SemaphoreType.DMA
        vmem = pl.BlockSpec(memory_space=pltpu.VMEM)
        return pl.pallas_call(
            functools.partial(solve_kernel, n_row, n_col),
            out_shape=(jax.ShapeDtypeStruct((rows, width), jnp.float32),) * 2,
            in_specs=[vmem] * 5,
            out_specs=(vmem, vmem),
            scratch_shapes=[
                pltpu.VMEM((n_col, sub, width), jnp.float32),
                pltpu.VMEM((n_row, sub, width), jnp.float32),
                pltpu.VMEM((2, n_col, rows, width), jnp.bfloat16),
                pltpu.VMEM((n_row * rows, n_col * rows), jnp.bfloat16),
                pltpu.VMEM((2, n_row, rows, width), SEND),
                pltpu.VMEM((2, n_row, rows, width), SEND),
                pltpu.VMEM((8, width), jnp.float32),
                pltpu.VMEM((2, n_row, 8, width), jnp.float32),
                pltpu.VMEM((2, n_col, 8, width), jnp.float32),
                dma((n_col, 2)),
                dma((n_row, 2)),
                dma((2, n_col, 2)),
                dma((2, n_row, 2)),
                dma((2, n_row, 2)),
                dma((2, n_col, 2)),
            ],
            compiler_params=pltpu.CompilerParams(collective_id=0, has_side_effects=True),
        )(observed, lengths.reshape(1, rows), features, length_scale.reshape(1, count),
          epoch_gain.reshape(1, width))

    placed = (P(("row", "col"), None), P(("row", "col")), P(("row", "col"), None), P(), P())
    return jax.shard_map(
        per_device,
        mesh=mesh,
        in_specs=placed,
        out_specs=(P(("row", "col"), None), P(("row", "col"), None)),
        check_vma=False,
    )
```

```python
import functools

import jax
import jax.numpy as jnp
from jax import lax
from jax.experimental import pallas as pl
from jax.experimental.pallas import tpu as pltpu
from jax.sharding import PartitionSpec as P

noise_level = 0.3
epoch_offset = 16.0
HIGHEST = lax.Precision.HIGHEST
VMEM_GRANT = 24 * 1024 * 1024


def solve_kernel(n_row, n_col, obs_ref, len_ref, feat_ref, scale_ref, gain_ref,
                 sol_ref, res_ref,
                 right, left, zbuf, wbuf, kmat, psend, precv, srow, scol,
                 feat_sem, left_sem, z_sem, w_sem, p_sem, srow_sem, scol_sem):
    rows, width = obs_ref.shape
    features = feat_ref.shape[0]
    pack = width // features
    sub = rows // pack
    my_row = lax.axis_index("row")
    my_col = lax.axis_index("col")

    def row_peer(shift):
        return {"row": lax.rem(my_row + shift, n_row)}

    def col_peer(shift):
        return {"col": lax.rem(my_col + shift, n_col)}

    def put(src, dst, sems, peer):
        copy = pltpu.make_async_remote_copy(
            src_ref=src, dst_ref=dst, send_sem=sems.at[0], recv_sem=sems.at[1],
            device_id=peer, device_id_type=pl.DeviceIdType.MESH)
        copy.start()
        return copy

    barrier = pltpu.get_barrier_semaphore()
    for shift in range(1, n_row):
        pl.semaphore_signal(barrier, inc=1, device_id=row_peer(shift), device_id_type=pl.DeviceIdType.MESH)
    for shift in range(1, n_col):
        pl.semaphore_signal(barrier, inc=1, device_id=col_peer(shift), device_id_type=pl.DeviceIdType.MESH)

    scaled = feat_ref[...].T / scale_ref[...]
    packed = jnp.concatenate([scaled[k * sub:(k + 1) * sub] for k in range(pack)], axis=1)
    right[0] = packed
    left[0] = packed

    at_row = lax.broadcasted_iota(jnp.int32, (rows, rows), 0)
    at_col = lax.broadcasted_iota(jnp.int32, (rows, rows), 1)
    spread = jnp.where(at_row == at_col, len_ref[...].astype(jnp.float32), 0.0)
    lengths = jnp.sum(spread, axis=1, keepdims=True)
    epoch = lax.broadcasted_iota(jnp.int32, (rows, width), 1).astype(jnp.float32)
    mask = (epoch < lengths).astype(jnp.float32)

    s = lax.broadcasted_iota(jnp.int32, (width, width), 0)
    t = lax.broadcasted_iota(jnp.int32, (width, width), 1)
    epoch_kernel = epoch_offset / ((s + t).astype(jnp.float32) + epoch_offset)
    epoch_kernel = epoch_kernel + jnp.where(s == t, gain_ref[...], 0.0)

    def mix(field):
        return jnp.dot(mask * field, epoch_kernel, precision=HIGHEST,
                       preferred_element_type=jnp.float32).astype(jnp.bfloat16)

    res0 = mask * obs_ref[...]
    wbuf[0, 0] = mix(res0)
    zbuf[0, 0] = res0

    pl.semaphore_wait(barrier, n_row - 1 + n_col - 1)

    pending = []
    right_copies = [put(right.at[0], right.at[d], feat_sem.at[d], col_peer(d)) for d in range(1, n_col)]
    left_copies = [put(left.at[0], left.at[d], left_sem.at[d], row_peer(d)) for d in range(1, n_row)]

    def send_w(step):
        return [put(wbuf.at[step, 0], wbuf.at[step, d], w_sem.at[step, d], col_peer(d)) for d in range(1, n_col)]

    w_copies = send_w(0)

    def send_z(step):
        return [put(zbuf.at[step, 0], zbuf.at[step, d], z_sem.at[step, d], row_peer(d)) for d in range(1, n_row)]

    z_copies = send_z(0)
    pending += w_copies + z_copies

    for copy in left_copies + right_copies:
        copy.wait_recv()
    pending += left_copies + right_copies

    lefts = left[...].reshape(n_row * sub, width)
    rolls = [lefts] + [pltpu.roll(lefts, k * features, 1) for k in range(1, pack)]
    group = lax.broadcasted_iota(jnp.int32, (sub, width), 1) // features
    stacked = []
    for k in range(pack):
        for d in range(n_row):
            for q in range(pack):
                piece = rolls[(k - q) % pack][d * sub:(d + 1) * sub]
                stacked.append(jnp.where(group == k, piece, 0.0))
    stacked = jnp.concatenate(stacked, axis=0)
    block = n_row * rows
    rights = right[...].reshape(n_col * sub, width)
    over = (((1,), (1,)), ((), ()))
    first = stacked[:block]
    left_sq = jnp.sum(first * first, axis=1, keepdims=True)
    picks_at = lax.broadcasted_iota(jnp.int32, (8, width), 0)
    picks = (lax.broadcasted_iota(jnp.int32, (8, width), 1) // features == picks_at).astype(jnp.float32)
    right_sq = lax.dot_general(picks, rights * rights, over, precision=HIGHEST,
                               preferred_element_type=jnp.float32)
    cross = lax.dot_general(stacked, rights, over, precision=HIGHEST,
                            preferred_element_type=jnp.float32)
    span = n_col * sub
    for k in range(pack):
        dist = jnp.maximum(left_sq + right_sq[k:k + 1] - 2.0 * cross[k * block:(k + 1) * block], 0.0)
        kmat[:, k * span:(k + 1) * span] = jnp.exp(-0.5 * dist).astype(jnp.bfloat16)

    def product(step, copies):
        for copy in copies:
            copy.wait_recv()
        pieces = [wbuf[step, d, k * sub:(k + 1) * sub] for k in range(pack) for d in range(n_col)]
        return jnp.dot(kmat[...], jnp.concatenate(pieces, axis=0), preferred_element_type=jnp.float32)

    def scatter(step, part):
        psend[step] = part.reshape(n_row, rows, width)
        return [put(psend.at[step, d], precv.at[step, d], p_sem.at[step, d], row_peer(n_row - d))
                for d in range(1, n_row)]

    def collect(step, sends):
        total = psend[step, 0]
        for d, copy in enumerate(sends, 1):
            copy.wait_recv()
            total = total + precv[step, d]
        return total

    lane_row = lax.broadcasted_iota(jnp.int32, (8, width), 0)

    def start_sums(step, one, two):
        srow[step, 0] = jnp.where(lane_row == 0, one, jnp.where(lane_row == 1, two, 0.0))
        return [put(srow.at[step, 0], srow.at[step, d], srow_sem.at[step, d], row_peer(d)) for d in range(1, n_row)]

    def relay_sums(step, copies):
        for copy in copies:
            copy.wait_recv()
        scol[step, 0] = jnp.sum(srow[step], axis=0)
        return [put(scol.at[step, 0], scol.at[step, d], scol_sem.at[step, d], col_peer(d)) for d in range(1, n_col)]

    def finish_sums(step, copies):
        for copy in copies:
            copy.wait_recv()
        total = jnp.sum(jnp.sum(scol[step], axis=0), axis=1, keepdims=True)
        return total[0:1], total[1:2]

    part = product(0, w_copies)
    p_copies = scatter(0, part)
    for copy in z_copies:
        copy.wait_recv()
    rows_all = n_row * rows
    own_norm = jnp.sum(res0 * res0, axis=0, keepdims=True)
    shared = jnp.sum(zbuf[0].reshape(rows_all, width) * part, axis=0, keepdims=True)
    row_copies = start_sums(0, own_norm, shared + noise_level * own_norm)
    pending += p_copies + row_copies
    image0 = mask * collect(0, p_copies) + noise_level * res0
    wbuf[1, 0] = mix(image0)
    w_copies = send_w(1)
    zbuf[1, 0] = mask * image0
    z_copies = send_z(1)
    col_copies = relay_sums(0, row_copies)
    pending += w_copies + z_copies + col_copies
    part = product(1, w_copies)
    for copy in z_copies:
        copy.wait_recv()
    norm0, curve0 = finish_sums(0, col_copies)
    alpha0 = norm0 / curve0
    res1 = res0 - alpha0 * image0
    masked1 = (zbuf[0] - alpha0 * zbuf[1]).reshape(rows_all, width)
    shared = jnp.sum(masked1 * part, axis=0, keepdims=True)
    along = jnp.sum(res1 * image0, axis=0, keepdims=True)
    own_norm = jnp.sum(res1 * res1, axis=0, keepdims=True)
    row_copies = start_sums(1, own_norm, along - alpha0 * (shared + noise_level * along))
    p_copies = scatter(1, part)
    col_copies = relay_sums(1, row_copies)
    pending += p_copies + row_copies + col_copies
    image00 = mask * collect(1, p_copies) + noise_level * image0
    image1 = image0 - alpha0 * image00
    norm1, curve1 = finish_sums(1, col_copies)
    ratio = norm1 / norm0
    alpha1 = norm1 / (curve1 - ratio * norm1 / alpha0)
    sol_ref[...] = alpha0 * res0 + alpha1 * (res1 + ratio * res0)
    res_ref[...] = res1 - alpha1 * (image1 + ratio * image0)
    for copy in pending:
        copy.wait_send()


def solution(mesh):
    n_row, n_col = mesh.shape["row"], mesh.shape["col"]

    def per_device(observed, lengths, features, length_scale, epoch_gain):
        rows, width = observed.shape
        count = features.shape[1]
        sub = rows * count // width
        dma = pltpu.SemaphoreType.DMA
        vmem = pl.BlockSpec(memory_space=pltpu.VMEM)
        return pl.pallas_call(
            functools.partial(solve_kernel, n_row, n_col),
            out_shape=(jax.ShapeDtypeStruct((rows, width), jnp.float32),) * 2,
            in_specs=[vmem] * 5,
            out_specs=(vmem, vmem),
            scratch_shapes=[
                pltpu.VMEM((n_col, sub, width), jnp.float32),
                pltpu.VMEM((n_row, sub, width), jnp.float32),
                pltpu.VMEM((2, n_row, rows, width), jnp.float32),
                pltpu.VMEM((2, n_col, rows, width), jnp.bfloat16),
                pltpu.VMEM((n_row * rows, n_col * rows), jnp.bfloat16),
                pltpu.VMEM((2, n_row, rows, width), jnp.float32),
                pltpu.VMEM((2, n_row, rows, width), jnp.float32),
                pltpu.VMEM((2, n_row, 8, width), jnp.float32),
                pltpu.VMEM((2, n_col, 8, width), jnp.float32),
                dma((n_col, 2)),
                dma((n_row, 2)),
                dma((2, n_row, 2)),
                dma((2, n_col, 2)),
                dma((2, n_row, 2)),
                dma((2, n_row, 2)),
                dma((2, n_col, 2)),
            ],
            compiler_params=pltpu.CompilerParams(
                collective_id=0, has_side_effects=True, vmem_limit_bytes=VMEM_GRANT),
        )(observed, lengths.reshape(1, rows), features.T, length_scale.reshape(1, count),
          epoch_gain.reshape(1, width))

    placed = (P(("row", "col"), None), P(("row", "col")), P(("row", "col"), None), P(), P())
    return jax.shard_map(
        per_device,
        mesh=mesh,
        in_specs=placed,
        out_specs=(P(("row", "col"), None), P(("row", "col"), None)),
        check_vma=False,
    )
```

```python
import functools

import jax
import jax.numpy as jnp
from jax import lax
from jax.experimental import pallas as pl
from jax.experimental.pallas import tpu as pltpu
from jax.sharding import PartitionSpec as P

noise_level = 0.3
epoch_offset = 16.0
HIGHEST = lax.Precision.HIGHEST
VMEM_GRANT = 55120 * 1024


def order(count):
    return sorted(range(1, count), key=lambda d: (-(d % 2), d))


def write_kernel(sol_ref, res_ref, sol_hbm, res_hbm, sems):
    copies = [pltpu.make_async_copy(sol_ref, sol_hbm, sems.at[0]), pltpu.make_async_copy(res_ref, res_hbm, sems.at[1])]
    for copy in copies:
        copy.start()
    for copy in copies:
        copy.wait()


def solve_kernel(n_row, n_col, obs_hbm, len_hbm, feat_hbm, scale_hbm, gain_hbm,
                 sol_ref, res_ref,
                 obs_ref, len_ref, feat_ref, scale_ref, gain_ref,
                 right, left, zbuf, wbuf, kmat, psend, precv, srow, scol, sall,
                 in_sem, feat_sem, left_sem, z_sem, w_sem, p_sem, srow_sem, scol_sem, sall_sem):
    rows, width = obs_ref.shape
    features = feat_ref.shape[0]
    pack = width // features
    sub = rows // pack
    my_row = lax.axis_index("row")
    my_col = lax.axis_index("col")

    def row_peer(shift):
        return {"row": lax.rem(my_row + shift, n_row)}

    def col_peer(shift):
        return {"col": lax.rem(my_col + shift, n_col)}

    def put(src, dst, sems, peer):
        copy = pltpu.make_async_remote_copy(
            src_ref=src, dst_ref=dst, send_sem=sems.at[0], recv_sem=sems.at[1],
            device_id=peer, device_id_type=pl.DeviceIdType.MESH)
        copy.start()
        return copy

    barrier = pltpu.get_barrier_semaphore()
    for shift in range(1, n_row):
        pl.semaphore_signal(barrier, inc=1, device_id=row_peer(shift), device_id_type=pl.DeviceIdType.MESH)
    for shift in range(1, n_col):
        pl.semaphore_signal(barrier, inc=1, device_id=col_peer(shift), device_id_type=pl.DeviceIdType.MESH)

    inputs = []
    for index, (src, dst) in enumerate(((feat_hbm, feat_ref), (scale_hbm, scale_ref), (obs_hbm, obs_ref),
                                        (len_hbm, len_ref), (gain_hbm, gain_ref))):
        inputs.append(pltpu.make_async_copy(src, dst, in_sem.at[index]))
        inputs[-1].start()
    for copy in inputs:
        copy.wait()
    scaled = feat_ref[...].T / scale_ref[...]
    packed = jnp.concatenate([scaled[k * sub:(k + 1) * sub] for k in range(pack)], axis=1)
    right[0] = packed
    left[0] = packed

    at_row = lax.broadcasted_iota(jnp.int32, (rows, rows), 0)
    at_col = lax.broadcasted_iota(jnp.int32, (rows, rows), 1)
    spread = jnp.where(at_row == at_col, len_ref[...].astype(jnp.float32), 0.0)
    lengths = jnp.sum(spread, axis=1, keepdims=True)
    epoch = lax.broadcasted_iota(jnp.int32, (rows, width), 1).astype(jnp.float32)
    mask = (epoch < lengths).astype(jnp.float32)

    s = lax.broadcasted_iota(jnp.int32, (width, width), 0)
    t = lax.broadcasted_iota(jnp.int32, (width, width), 1)
    epoch_kernel = epoch_offset / ((s + t).astype(jnp.float32) + epoch_offset)
    epoch_kernel = epoch_kernel + jnp.where(s == t, gain_ref[...], 0.0)

    def mix(field):
        return jnp.dot(mask * field, epoch_kernel, precision=HIGHEST,
                       preferred_element_type=jnp.float32).astype(jnp.bfloat16)

    res0 = mask * obs_ref[...]
    wbuf[0, 0] = mix(res0)
    zbuf[0, 0] = res0

    pl.semaphore_wait(barrier, n_row - 1 + n_col - 1)

    pending = []
    right_copies = [put(right.at[0], right.at[d], feat_sem.at[d], col_peer(d)) for d in order(n_col)]
    left_copies = [put(left.at[0], left.at[d], left_sem.at[d], row_peer(d)) for d in range(1, n_row)]

    def send_w(step):
        return [put(wbuf.at[step, 0], wbuf.at[step, d], w_sem.at[step, d], col_peer(d)) for d in order(n_col)]

    w_copies = send_w(0)

    def send_z(step):
        return [put(zbuf.at[step, 0], zbuf.at[step, d], z_sem.at[step, d], row_peer(d)) for d in range(1, n_row)]

    z_copies = send_z(0)
    pending += w_copies + z_copies

    for copy in left_copies + right_copies:
        copy.wait_recv()
    pending += left_copies + right_copies

    lefts = left[...].reshape(n_row * sub, width)
    rolls = [lefts] + [pltpu.roll(lefts, k * features, 1) for k in range(1, pack)]
    group = lax.broadcasted_iota(jnp.int32, (sub, width), 1) // features
    stacked = []
    for k in range(pack):
        for d in range(n_row):
            for q in range(pack):
                piece = rolls[(k - q) % pack][d * sub:(d + 1) * sub]
                stacked.append(jnp.where(group == k, piece, 0.0))
    stacked = jnp.concatenate(stacked, axis=0)
    block = n_row * rows
    rights = right[...].reshape(n_col * sub, width)
    over = (((1,), (1,)), ((), ()))
    first = stacked[:block]
    left_sq = jnp.sum(first * first, axis=1, keepdims=True)
    picks_at = lax.broadcasted_iota(jnp.int32, (8, width), 0)
    picks = (lax.broadcasted_iota(jnp.int32, (8, width), 1) // features == picks_at).astype(jnp.float32)
    right_sq = lax.dot_general(picks, rights * rights, over, precision=HIGHEST,
                               preferred_element_type=jnp.float32)
    cross = lax.dot_general(stacked, rights, over, precision=HIGHEST,
                            preferred_element_type=jnp.float32)
    span = n_col * sub
    for k in range(pack):
        dist = jnp.maximum(left_sq + right_sq[k:k + 1] - 2.0 * cross[k * block:(k + 1) * block], 0.0)
        kmat[:, k * span:(k + 1) * span] = jnp.exp(-0.5 * dist).astype(jnp.bfloat16)

    def product(step, copies):
        for copy in copies:
            copy.wait_recv()
        pieces = [wbuf[step, d, k * sub:(k + 1) * sub] for k in range(pack) for d in range(n_col)]
        return jnp.dot(kmat[...], jnp.concatenate(pieces, axis=0), preferred_element_type=jnp.float32)

    def scatter(step, part):
        psend[step] = part.reshape(n_row, rows, width)
        return [put(psend.at[step, d], precv.at[step, d], p_sem.at[step, d], row_peer(n_row - d))
                for d in range(1, n_row)]

    def collect(step, sends):
        total = psend[step, 0]
        for d, copy in enumerate(sends, 1):
            copy.wait_recv()
            total = total + precv[step, d]
        return total

    lanes = lax.broadcasted_iota(jnp.int32, (1, width), 1)
    half = width // 2

    def pair_row(one, two):
        return jnp.where(lanes < half, one + pltpu.roll(one, half, 1), two + pltpu.roll(two, half, 1))

    def start_sums(row):
        srow[0] = row
        return [put(srow.at[0], srow.at[d], srow_sem.at[d], row_peer(d)) for d in range(1, n_row)]

    def relay_sums(copies):
        for copy in copies:
            copy.wait_recv()
        scol[0] = jnp.sum(srow[...], axis=0)
        return [put(scol.at[0], scol.at[d], scol_sem.at[d], col_peer(d)) for d in order(n_col)]

    def direct_sums(row):
        sall[0] = row
        copies = []
        for d in order(n_col) + [0]:
            for e in range(n_row):
                if d or e:
                    slot = d * n_row + e
                    copies.append(put(sall.at[0], sall.at[slot], sall_sem.at[slot], {**row_peer(e), **col_peer(d)}))
        return copies

    def finish_sums(buffer, copies):
        for copy in copies:
            copy.wait_recv()
        total = jnp.sum(buffer[...], axis=0)
        return (jnp.sum(jnp.where(lanes < half, total, 0.0), axis=1, keepdims=True),
                jnp.sum(jnp.where(lanes < half, 0.0, total), axis=1, keepdims=True))

    part = product(0, w_copies)
    for copy in z_copies:
        copy.wait_recv()
    rows_all = n_row * rows
    own_norm = jnp.sum(res0 * res0, axis=0, keepdims=True)
    shared = jnp.sum(zbuf[0].reshape(rows_all, width) * part, axis=0, keepdims=True)
    row_copies = start_sums(pair_row(own_norm, shared + noise_level * own_norm))
    p_copies = scatter(0, part)
    col_copies = relay_sums(row_copies)
    pending += p_copies + row_copies + col_copies
    image0 = mask * collect(0, p_copies) + noise_level * res0
    wbuf[1, 0] = mix(image0)
    w_copies = send_w(1)
    zbuf[1, 0] = mask * image0
    z_copies = send_z(1)
    pending += w_copies + z_copies
    part = product(1, w_copies)
    for copy in z_copies:
        copy.wait_recv()
    norm0, curve0 = finish_sums(scol, col_copies)
    alpha0 = norm0 / curve0
    res1 = res0 - alpha0 * image0
    masked1 = (zbuf[0] - alpha0 * zbuf[1]).reshape(rows_all, width)
    shared = jnp.sum(masked1 * part, axis=0, keepdims=True)
    along = jnp.sum(res1 * image0, axis=0, keepdims=True)
    own_norm = jnp.sum(res1 * res1, axis=0, keepdims=True)
    all_copies = direct_sums(pair_row(own_norm, along - alpha0 * (shared + noise_level * along)))
    p_copies = scatter(1, part)
    pending += p_copies + all_copies
    image00 = mask * collect(1, p_copies) + noise_level * image0
    image1 = image0 - alpha0 * image00
    for copy in pending:
        copy.wait_send()
    norm1, curve1 = finish_sums(sall, all_copies)
    ratio = norm1 / norm0
    alpha1 = norm1 / (curve1 - ratio * norm1 / alpha0)
    sol_ref[...] = alpha0 * res0 + alpha1 * (res1 + ratio * res0)
    res_ref[...] = res1 - alpha1 * (image1 + ratio * image0)


def solution(mesh):
    n_row, n_col = mesh.shape["row"], mesh.shape["col"]

    def per_device(observed, lengths, features, length_scale, epoch_gain):
        rows, width = observed.shape
        count = features.shape[1]
        sub = rows * count // width
        dma = pltpu.SemaphoreType.DMA
        hbm = pl.BlockSpec(memory_space=pltpu.HBM)
        vmem = pl.BlockSpec(memory_space=pltpu.VMEM)
        results = pl.pallas_call(
            functools.partial(solve_kernel, n_row, n_col),
            out_shape=(jax.ShapeDtypeStruct((rows, width), jnp.float32),) * 2,
            in_specs=[hbm] * 5,
            out_specs=(vmem, vmem),
            scratch_shapes=[
                pltpu.VMEM((rows, width), jnp.float32),
                pltpu.VMEM((1, rows), jnp.int32),
                pltpu.VMEM((count, rows), jnp.float32),
                pltpu.VMEM((1, count), jnp.float32),
                pltpu.VMEM((1, width), jnp.float32),
                pltpu.VMEM((n_col, sub, width), jnp.float32),
                pltpu.VMEM((n_row, sub, width), jnp.float32),
                pltpu.VMEM((2, n_row, rows, width), jnp.float32),
                pltpu.VMEM((2, n_col, rows, width), jnp.bfloat16),
                pltpu.VMEM((n_row * rows, n_col * rows), jnp.bfloat16),
                pltpu.VMEM((2, n_row, rows, width), jnp.float32),
                pltpu.VMEM((2, n_row, rows, width), jnp.float32),
                pltpu.VMEM((n_row, 1, width), jnp.float32),
                pltpu.VMEM((n_col, 1, width), jnp.float32),
                pltpu.VMEM((n_row * n_col, 1, width), jnp.float32),
                dma((5,)),
                dma((n_col, 2)),
                dma((n_row, 2)),
                dma((2, n_row, 2)),
                dma((2, n_col, 2)),
                dma((2, n_row, 2)),
                dma((n_row, 2)),
                dma((n_col, 2)),
                dma((n_row * n_col, 2)),
            ],
            compiler_params=pltpu.CompilerParams(
                collective_id=0, has_side_effects=True, vmem_limit_bytes=VMEM_GRANT),
        )(observed, lengths.reshape(1, rows), features.T, length_scale.reshape(1, count),
          epoch_gain.reshape(1, width))
        return pl.pallas_call(
            write_kernel,
            out_shape=(jax.ShapeDtypeStruct((rows, width), jnp.float32),) * 2,
            in_specs=[vmem] * 2,
            out_specs=(hbm, hbm),
            scratch_shapes=[dma((2,))],
            compiler_params=pltpu.CompilerParams(vmem_limit_bytes=VMEM_GRANT),
        )(*results)

    placed = (P(("row", "col"), None), P(("row", "col")), P(("row", "col"), None), P(), P())
    return jax.shard_map(
        per_device,
        mesh=mesh,
        in_specs=placed,
        out_specs=(P(("row", "col"), None), P(("row", "col"), None)),
        check_vma=False,
    )
```
